32 devices in a mesh: src: 8 (over y, x, core), dst: 4 (over z).
Axes of the slice: x: 2, y: 2, z: 4, core: 2. Of those that a mesh axis runs over, the one named last changes fastest.
Arguments:
- raw: bfloat16 [4096, 256], P(('src', 'dst')), may hold values from -6 to 6
- enc_w1: bfloat16 [256, 512], replicated, may hold values from -0.375 to 0.375
- enc_w2: bfloat16 [512, 256], replicated, may hold values from -0.25 to 0.25
- block_weights: float32 [512, 128, 128], P(('src', 'dst')), may hold values from -0.125 to 0.125
- block_cols: int32 [512], P(('src', 'dst')), may hold values from 0 to 3, as said below
- noise: bfloat16 [3, 4096, 256], P(None, ('src', 'dst')), may hold values from -3 to 3
Outputs:
- encoded: bfloat16 [4096, 256], P(('src', 'dst'))
- hops: bfloat16 [3, 4096, 256], P(None, ('src', 'dst'))
The draws below stay inside these ranges and needn't reach their ends.
Inputs may be any that keep to these rules, and one draw needn't show every extreme that they name: `block_cols`: entry b of each device's 16 entries belongs to row block b // 2; row blocks 2j and 2j+1 of a device together name every column block exactly once, each naming 4 // 2 distinct ones.
All inputs are finite; a program needn't handle non-finite values.
Results may differ from the reference program's by a relative error of at most 0.0058.
Values may be sent and summed in bfloat16 or wider, within the bound.
A program may use at most 128 MiB of HBM per device.

```python
import jax
import jax.numpy as jnp
from jax import lax

F_IN = 256
HID = 512
W = 256
BS = 128
HOPS = 3
ROWS_DEV = 128
NODES = 4096
GR = 8
GC = 4
BLK_DEV = 16
BLOCKS = 512
N_SRC = 8
N_DST = 4


def draw_block_cols(key, part):
    pairs = N_SRC * N_DST * (GR // 2)
    keys = jax.random.split(jax.random.fold_in(key, 7), pairs)
    perms = jax.vmap(lambda sub: jax.random.permutation(sub, GC))(keys)
    return perms.reshape(BLOCKS).astype(jnp.int32)


def block_scale(rng, dims, pieces, smallest, largest):
    def one(position, blocks):
        draws = jax.random.uniform(jax.random.fold_in(jax.random.fold_in(rng, 6), position), (blocks,), jnp.float32, smallest / len(pieces), largest / len(pieces))
        return jnp.repeat(jnp.exp(draws), dims[position] // blocks).reshape((-1,) + (1,) * (len(dims) - position - 1))

    gain = one(*pieces[0])
    for cut in pieces[1:]:
        gain = gain * one(*cut)
    return gain


def centred(key, dims, deviation, limit, cuts=(), kind=jnp.bfloat16):
    result = deviation * jax.random.normal(key, dims, jnp.float32)
    if cuts:
        result = result * block_scale(key, dims, cuts, -0.22, 0.18)
    return jnp.clip(result, -limit, limit).astype(kind)


def setup_inputs(seed: int = 0) -> dict:
    key_list = jax.random.split(jax.random.key(seed), 7)
    raw = centred(key_list[0], (NODES, F_IN), 1.0, 6.0, ((0, 32),))
    enc_w1 = centred(key_list[1], (F_IN, HID), F_IN ** -0.5, 0.375)
    enc_w2 = centred(key_list[2], (HID, W), HID ** -0.5, 0.25)
    block_weights = centred(key_list[3], (BLOCKS, BS, BS), (N_SRC * N_DST * ROWS_DEV // 2) ** -0.5, 0.125, ((0, 32),), jnp.float32)
    block_cols = draw_block_cols(jax.random.fold_in(key_list[6], 71), 0)
    noise = centred(key_list[5], (HOPS, NODES, W), 0.5, 3.0, ((1, 32),))
    return {"raw": raw, "enc_w1": enc_w1, "enc_w2": enc_w2, "block_weights": block_weights, "block_cols": block_cols, "noise": noise}


def normalize_rows(z):
    return (z * lax.rsqrt(lax.optimization_barrier(jnp.mean(z * z, axis=-1, keepdims=True)) + 1e-06)).astype(jnp.bfloat16)

def reference(raw, enc_w1, enc_w2, block_weights, block_cols, noise):
    hidden = jax.nn.silu(jnp.dot(raw, enc_w1, preferred_element_type=jnp.float32)).astype(jnp.bfloat16)
    encoded = normalize_rows(jnp.dot(hidden, enc_w2, preferred_element_type=jnp.float32))
    weights = block_weights.reshape(N_SRC, N_DST, BLK_DEV, BS, BS)
    columns = block_cols.reshape(N_SRC, N_DST, BLK_DEV)
    half = GC // 2
    feats = encoded
    kept = []
    for step in range(HOPS):
        col_blocks = feats.astype(jnp.float32).reshape(N_SRC, GC, BS, W)

        def one_dest(dest):
            w_dest = lax.dynamic_index_in_dim(weights, dest, 1, keepdims=False)
            c_dest = lax.dynamic_index_in_dim(columns, dest, 1, keepdims=False)
            fetched = jax.vmap(lambda blocks, cols: jnp.take(blocks, cols, axis=0))(col_blocks, c_dest)
            prods = jnp.einsum('sbij,sbjw->sbiw', w_dest, fetched, precision=lax.Precision.HIGHEST)
            return prods.reshape(N_SRC, GR, half, BS, W).sum(axis=(0, 2)).reshape(N_SRC, ROWS_DEV, W)
        agg = lax.map(one_dest, jnp.arange(N_DST, dtype=jnp.int32))
        agg = jnp.transpose(agg, (1, 0, 2, 3)).reshape(NODES, W)
        feats = normalize_rows(agg + noise[step].astype(jnp.float32))
        kept.append(feats)
    return (encoded, jnp.stack(kept))
```

```python
import functools

import jax
import jax.numpy as jnp
from jax import lax
from jax.experimental import pallas as pl
from jax.experimental.pallas import tpu as pltpu
from jax.sharding import PartitionSpec as P

MESH = pl.DeviceIdType.MESH
F32 = jnp.float32
BF16 = jnp.bfloat16


def shifted(me, step, count):
    if count & (count - 1) == 0:
        return me ^ step, me ^ step
    return lax.rem(me + step, count), lax.rem(me + count - step, count)


def kernel(
    n_src, n_dst, hops,
    raw_h, w1_h, w2_h, bw_h, cols, noise_h,
    enc_h, hops_h,
    raw_v, w1_v, w2_v, bw_v, noise_v, enc_v, last_v,
    dense, scaled, gath, cross, acc, out, inn, near_out, near_in,
    noise_p, zs, stat_out, stat_in, scale, kept, kept_in,
    load_sem, store_sem, w_send, w_recv, g_send, g_recv, r_send, r_recv, s_send, s_recv, p_send, p_recv,
):
    src, dst = lax.axis_index("src"), lax.axis_index("dst")
    pairs = n_src // 2
    pair, core = src // 2, lax.rem(src, 2)
    partner = pair * 2 + 1 - core
    side = bw_v.shape[1]
    per_row = bw_v.shape[0] // n_src
    rows, width = enc_v.shape
    half = width // 2
    last = hops - 1

    def at_core(chip, rel):
        return chip * 2 + (1 - core if rel else core)

    def lanes(h):
        return pl.ds(pl.multiple_of(h * half, half), half)

    def remote(a, b, send, recv, to):
        return pltpu.make_async_remote_copy(
            src_ref=a, dst_ref=b, send_sem=send, recv_sem=recv, device_id=to, device_id_type=MESH
        )

    loads = [
        pltpu.make_async_copy(a, b, load_sem.at[i])
        for i, (a, b) in enumerate(
            ((raw_h, raw_v), (w1_h, w1_v), (w2_h, w2_v), (bw_h, bw_v), (noise_h, noise_v))
        )
    ]
    for load in loads:
        load.start()

    to_dst = [shifted(dst, step, n_dst)[0] if step else dst for step in range(n_dst)]
    from_dst = [shifted(dst, step, n_dst)[1] if step else dst for step in range(n_dst)]
    to_pair = [shifted(pair, step, pairs)[0] if step else pair for step in range(pairs)]

    barrier = pltpu.get_barrier_semaphore()
    greeted = 0
    greet = [{"src": partner}]
    for rel in (0, 1):
        greet += [{"src": at_core(pair, rel), "dst": to} for to in to_dst[1:]]
        greet += [{"src": at_core(to, rel)} for to in to_pair[1:]]
    for to in greet:
        pl.semaphore_signal(barrier, inc=1, device_id=to, device_id_type=MESH)
        greeted += 1

    def normalized(z):
        root = lax.rsqrt(jnp.sum(z * z, axis=-1, keepdims=True) * (1.0 / width) + 1e-06)
        return (z * root).astype(BF16)

    sent = []

    def start(copy):
        copy.start()
        sent.append(copy)
        return copy

    far_first = list(reversed(range(1, n_dst)))

    loads[0].wait()
    loads[1].wait()
    v = jnp.dot(raw_v[...], w1_v[...], preferred_element_type=F32)
    hidden = (v * jax.nn.sigmoid(v)).astype(BF16)
    loads[2].wait()
    feats = normalized(jnp.dot(hidden, w2_v[...], preferred_element_type=F32))
    mine = jnp.where(core == 0, feats[:, :half], feats[:, half:])
    gath[0, dst, core] = mine
    cross[...] = jnp.where(core == 0, feats[:, half:], feats[:, :half])
    pl.semaphore_wait(barrier, greeted)
    first = {}
    for step, rel in [(step, rel) for step in far_first for rel in (0, 1)] + [(0, 1)]:
        first[step, rel] = start(
            remote(
                cross if rel else gath.at[0, dst, core],
                gath.at[0, dst, core],
                g_send.at[0, step, rel],
                g_recv.at[0, step, rel],
                {"src": at_core(pair, rel), "dst": to_dst[step]},
            )
        )
    enc_v[...] = feats
    stores = [pltpu.make_async_copy(enc_v, enc_h, store_sem.at[0])]
    stores[0].start()

    loads[3].wait()
    weights = []
    blocks = [[bw_v[r * per_row + i].astype(BF16) for i in range(per_row)] for r in range(n_src)]
    for step in range(n_dst):
        c = from_dst[step]
        for r in range(n_src):
            total = None
            for i in range(per_row):
                term = jnp.where(cols[r * per_row + i] == c, blocks[r][i], jnp.zeros_like(blocks[r][i]))
                total = term if total is None else total + term
            dense[c, core, r] = total
        weights.append(
            start(
                remote(
                    dense.at[c, core], dense.at[c, core], w_send.at[step], w_recv.at[step], {"src": partner}
                )
            )
        )
    loads[4].wait()
    if hops > 1:
        noise_copy = start(
            remote(
                noise_v.at[pl.ds(0, last), :, lanes(1 - core)],
                noise_p,
                p_send.at[3 * hops],
                p_recv.at[3 * hops],
                {"src": partner},
            )
        )

    ones = jnp.ones((8, half), BF16)

    def row_sums(z):
        squares = z * z
        high = squares.astype(BF16)
        low = (squares - high.astype(F32)).astype(BF16)
        dims = (((1,), (1,)), ((), ()))
        return lax.dot_general(ones, high, dims, preferred_element_type=F32) + lax.dot_general(
            ones, low, dims, preferred_element_type=F32
        )

    data = {}
    scales = {}
    pending = None
    scatter_steps = list(reversed(range(1, pairs))) + [0]
    for hop in range(hops):
        for step in range(n_dst):
            c = from_dst[step]
            if hop == 0:
                weights[step].wait_recv()
            else:
                if step:
                    scales[hop, step].wait_recv()
                by = jnp.concatenate([scale[hop - 1, c, 0, 0:1], scale[hop - 1, c, 1, 0:1]], axis=1)
                for r in range(n_src):
                    w = jnp.concatenate([dense[c, 0, r], dense[c, 1, r]], axis=1)
                    scaled[r] = (w.astype(F32) * by).astype(BF16)
            for u in (0, 1):
                if hop == 0:
                    if step or u:
                        first[step, u].wait_recv()
                elif step:
                    data[hop, step, u].wait_recv()
            f = jnp.concatenate([gath[hop, c, 0], gath[hop, c, 1]], axis=0)

            def product(r):
                w = scaled[r] if hop else jnp.concatenate([dense[c, 0, r], dense[c, 1, r]], axis=1)
                return jnp.dot(w, f, preferred_element_type=F32)

            if step < n_dst - 1:
                for r in range(n_src):
                    y = product(r)
                    acc[r] = y if step == 0 else acc[r] + y
            if step == 0 and pending is not None:
                pending()
                pending = None
        copies = {}
        for u in (0, 1):
            for step in scatter_steps:
                to = to_pair[step]
                if hop < last:
                    r = to * 2 + u
                    y = product(r) + acc[r]
                    if step == 0:
                        near_in[u] = y
                        continue
                    out[hop, step - 1, u] = y.astype(BF16)
                    copies[step, u] = start(
                        remote(
                            out.at[hop, step - 1, u],
                            inn.at[hop, step - 1, u],
                            r_send.at[hop, step - 1, u],
                            r_recv.at[hop, step - 1, u],
                            {"src": at_core(to, 0)},
                        )
                    )
                    continue
                rel = 1 - u
                r = at_core(to, rel)
                y = product(r) + acc[r]
                if step == 0 and rel == 0:
                    zs[core] = y
                elif step == 0:
                    near_out[...] = y
                    copies[0, 1] = start(
                        remote(
                            near_out, zs.at[core], p_send.at[3 * hops + 1], p_recv.at[3 * hops + 1], {"src": partner}
                        )
                    )
                else:
                    out[hop, step - 1, rel] = y.astype(BF16)
                    copies[step, rel] = start(
                        remote(
                            out.at[hop, step - 1, rel],
                            inn.at[hop, step - 1, core],
                            r_send.at[hop, step - 1, rel],
                            r_recv.at[hop, step - 1, rel],
                            {"src": r},
                        )
                    )
        if hop == last:
            for copy in copies.values():
                copy.wait_recv()
            sums = []
            for h in range(2):
                z = zs[h] + noise_v[hop, :, h * half : (h + 1) * half].astype(F32)
                for step in range(1, pairs):
                    z = z + inn[hop, step - 1, h].astype(F32)
                sums.append(z)
            last_v[...] = normalized(jnp.concatenate(sums, axis=1))
            stores.append(pltpu.make_async_copy(last_v, hops_h.at[hop], store_sem.at[1]))
            stores[-1].start()
            continue
        if hop == 0:
            noise_copy.wait_recv()
        z_values = []
        for u in (0, 1):
            own_noise = noise_v[hop, :, lanes(core)]
            z = near_in[u] + jnp.where(core == u, own_noise, noise_p[hop]).astype(F32)
            for step in range(1, pairs):
                copies[step, u].wait_recv()
                z = z + inn[hop, step - 1, u].astype(F32)
            gath[hop + 1, dst, u] = z.astype(BF16)
            for step in far_first:
                data[hop + 1, step, u] = start(
                    remote(
                        gath.at[hop + 1, dst, u],
                        gath.at[hop + 1, dst, u],
                        g_send.at[hop + 1, step, u],
                        g_recv.at[hop + 1, step, u],
                        {"dst": to_dst[step]},
                    )
                )
            zs[u] = z
            stat_out[hop, u] = row_sums(z)
        stats = start(
            remote(stat_out.at[hop], stat_in.at[hop], p_send.at[hop], p_recv.at[hop], {"src": partner})
        )
        stats.wait_recv()
        scale[hop, dst] = lax.rsqrt((stat_out[hop] + stat_in[hop]) * (1.0 / width) + 1e-06)
        for step in far_first:
            scales[hop + 1, step] = start(
                remote(
                    scale.at[hop, dst],
                    scale.at[hop, dst],
                    s_send.at[hop, step],
                    s_recv.at[hop, step],
                    {"dst": to_dst[step]},
                )
            )

        def pending(hop=hop):
            for u in (0, 1):
                column = jnp.transpose(jnp.broadcast_to(scale[hop, dst, u, 0:1], (rows, rows)))
                kept[hop, u] = (zs[u] * column).astype(BF16)
            copy = start(
                remote(
                    kept.at[hop, 1 - core],
                    kept_in.at[hop],
                    p_send.at[hops + hop],
                    p_recv.at[hops + hop],
                    {"src": partner},
                )
            )
            store = pltpu.make_async_copy(
                kept.at[hop, core], hops_h.at[hop, :, lanes(core)], store_sem.at[2 + 2 * hop]
            )
            store.start()
            stores.append(store)
            copy.wait_recv()
            store = pltpu.make_async_copy(
                kept_in.at[hop], hops_h.at[hop, :, lanes(1 - core)], store_sem.at[3 + 2 * hop]
            )
            store.start()
            stores.append(store)

    for copy in sent:
        copy.wait_send()
    for store in stores:
        store.wait()


def finish(enc_i, hops_i, enc_o, hops_o, enc_v, hops_v, sem):
    reads = [
        pltpu.make_async_copy(hops_i, hops_v, sem.at[0]),
        pltpu.make_async_copy(enc_i, enc_v, sem.at[1]),
    ]
    writes = [
        pltpu.make_async_copy(hops_v, hops_o, sem.at[2]),
        pltpu.make_async_copy(enc_v, enc_o, sem.at[3]),
    ]
    for read in reads:
        read.start()
    for read, write in zip(reads, writes):
        read.wait()
        write.start()
    for write in writes:
        write.wait()


def shards(n_src, n_dst, raw, enc_w1, enc_w2, block_weights, block_cols, noise):
    blocks, side, _ = block_weights.shape
    hops, rows, width = noise.shape
    pairs = n_src // 2
    half = width // 2
    assert rows == side and n_src % 2 == 0
    anywhere = pl.BlockSpec(memory_space=pl.ANY)
    dma = pltpu.SemaphoreType.DMA
    far = max(pairs - 1, 1)
    mid = max(hops - 1, 1)
    encoded, kept = pl.pallas_call(
        functools.partial(kernel, n_src, n_dst, hops),
        out_shape=(
            jax.ShapeDtypeStruct((rows, width), BF16),
            jax.ShapeDtypeStruct((hops, rows, width), BF16),
        ),
        in_specs=[anywhere] * 4 + [pl.BlockSpec(memory_space=pltpu.SMEM), anywhere],
        out_specs=(anywhere, anywhere),
        scratch_shapes=[
            pltpu.VMEM(raw.shape, BF16),
            pltpu.VMEM(enc_w1.shape, BF16),
            pltpu.VMEM(enc_w2.shape, BF16),
            pltpu.VMEM(block_weights.shape, F32),
            pltpu.VMEM(noise.shape, BF16),
            pltpu.VMEM((rows, width), BF16),
            pltpu.VMEM((rows, width), BF16),
            pltpu.VMEM((n_dst, 2, n_src, side, side), BF16),
            pltpu.VMEM((n_src, side, 2 * side), BF16),
            pltpu.VMEM((hops, n_dst, 2, rows, half), BF16),
            pltpu.VMEM((rows, half), BF16),
            pltpu.VMEM((n_src, rows, half), F32),
            pltpu.VMEM((hops, far, 2, rows, half), BF16),
            pltpu.VMEM((hops, far, 2, rows, half), BF16),
            pltpu.VMEM((rows, half), F32),
            pltpu.VMEM((2, rows, half), F32),
            pltpu.VMEM((mid, rows, half), BF16),
            pltpu.VMEM((2, rows, half), F32),
            pltpu.VMEM((mid, 2, 8, rows), F32),
            pltpu.VMEM((mid, 2, 8, rows), F32),
            pltpu.VMEM((mid, n_dst, 2, 8, rows), F32),
            pltpu.VMEM((mid, 2, rows, half), BF16),
            pltpu.VMEM((mid, rows, half), BF16),
            dma((5,)),
            dma((2 + 2 * hops,)),
            dma((n_dst,)),
            dma((n_dst,)),
            dma((hops, n_dst, 2)),
            dma((hops, n_dst, 2)),
            dma((hops, far, 2)),
            dma((hops, far, 2)),
            dma((mid, n_dst)),
            dma((mid, n_dst)),
            dma((3 * hops + 2,)),
            dma((3 * hops + 2,)),
        ],
        compiler_params=pltpu.CompilerParams(
            collective_id=0, has_side_effects=True, vmem_limit_bytes=60 * 1024 * 1024
        ),
    )(raw, enc_w1, enc_w2, block_weights, block_cols, noise)
    shapes = (
        jax.ShapeDtypeStruct((rows, width), BF16),
        jax.ShapeDtypeStruct((hops, rows, width), BF16),
    )
    return pl.pallas_call(
        finish,
        out_shape=shapes,
        in_specs=[anywhere, anywhere],
        out_specs=(anywhere, anywhere),
        scratch_shapes=[pltpu.VMEM(s.shape, BF16) for s in shapes] + [dma((4,))],
    )(encoded, kept)


def solution(mesh):
    placed = (
        P(("src", "dst"), None),
        P(),
        P(),
        P(("src", "dst"), None, None),
        P(("src", "dst")),
        P(None, ("src", "dst"), None),
    )
    return jax.shard_map(
        functools.partial(shards, mesh.shape["src"], mesh.shape["dst"]),
        mesh=mesh,
        in_specs=placed,
        out_specs=(P(("src", "dst"), None), P(None, ("src", "dst"), None)),
        check_vma=False,
    )
```

```python
import functools

import jax
import jax.numpy as jnp
from jax import lax
from jax.experimental import pallas as pl
from jax.experimental.pallas import tpu as pltpu
from jax.sharding import PartitionSpec as P

MESH = pl.DeviceIdType.MESH
F32 = jnp.float32
BF16 = jnp.bfloat16


def shifted(me, step, count):
    if count & (count - 1) == 0:
        return me ^ step, me ^ step
    return lax.rem(me + step, count), lax.rem(me + count - step, count)


def kernel(
    n_src, n_dst, hops,
    raw_h, w1_h, w2_h, bw_h, cols_h, noise_h,
    enc_v, hops_v,
    raw_v, w1_v, w2_v, bw_v, noise_v, cols,
    dense, scaled, gath, cross, acc, out, inn, near_out, near_in,
    noise_p, zs, ends, stat_out, stat_in, scale, kept, kept_in,
    load_sem, w_send, w_recv, g_send, g_recv, r_send, r_recv, s_send, s_recv, p_send, p_recv,
):
    src, dst = lax.axis_index("src"), lax.axis_index("dst")
    pairs = n_src // 2
    pair, core = src // 2, lax.rem(src, 2)
    partner = pair * 2 + 1 - core
    side = bw_v.shape[1]
    per_row = bw_v.shape[0] // n_src
    rows, width = enc_v.shape
    half = width // 2
    last = hops - 1

    def at_core(chip, rel):
        return chip * 2 + (1 - core if rel else core)

    def lanes(h):
        return pl.ds(pl.multiple_of(h * half, half), half)

    def remote(a, b, send, recv, to):
        return pltpu.make_async_remote_copy(
            src_ref=a, dst_ref=b, send_sem=send, recv_sem=recv, device_id=to, device_id_type=MESH
        )

    loads = [
        pltpu.make_async_copy(a, b, load_sem.at[i])
        for i, (a, b) in enumerate(
            (
                (raw_h, raw_v),
                (w1_h, w1_v),
                (w2_h, w2_v),
                (bw_h, bw_v),
                (noise_h, noise_v),
                (cols_h, cols),
            )
        )
    ]
    for load in loads:
        load.start()

    to_dst = [shifted(dst, step, n_dst)[0] if step else dst for step in range(n_dst)]
    from_dst = [shifted(dst, step, n_dst)[1] if step else dst for step in range(n_dst)]
    to_pair = [shifted(pair, step, pairs)[0] if step else pair for step in range(pairs)]

    barrier = pltpu.get_barrier_semaphore()
    greeted = 0
    greet = [{"src": partner}]
    for rel in (0, 1):
        greet += [{"src": at_core(pair, rel), "dst": to} for to in to_dst[1:]]
        greet += [{"src": at_core(to, rel)} for to in to_pair[1:]]
    for to in greet:
        pl.semaphore_signal(barrier, inc=1, device_id=to, device_id_type=MESH)
        greeted += 1

    def normalized(z):
        root = lax.rsqrt(jnp.sum(z * z, axis=-1, keepdims=True) * (1.0 / width) + 1e-06)
        return (z * root).astype(BF16)

    sent = []

    def start(copy):
        copy.start()
        sent.append(copy)
        return copy

    middle = [n_dst // 2] if n_dst > 1 else []
    rest = [step for step in range(1, n_dst) if step not in middle]
    far_first = list(reversed(range(1, n_dst)))

    loads[0].wait()
    loads[1].wait()
    v = jnp.dot(raw_v[...], w1_v[...], preferred_element_type=F32)
    hidden = (v * jax.nn.sigmoid(v)).astype(BF16)
    loads[2].wait()
    feats = normalized(jnp.dot(hidden, w2_v[...], preferred_element_type=F32))
    mine = jnp.where(core == 0, feats[:, :half], feats[:, half:])
    gath[0, dst, core] = mine
    cross[...] = jnp.where(core == 0, feats[:, half:], feats[:, :half])
    pl.semaphore_wait(barrier, greeted)
    first = {}
    for step, rel in [(step, rel) for step in middle + rest[::-1] for rel in (1, 0)] + [(0, 1)]:
        first[step, rel] = start(
            remote(
                cross if rel else gath.at[0, dst, core],
                gath.at[0, dst, core],
                g_send.at[0, step, rel],
                g_recv.at[0, step, rel],
                {"src": at_core(pair, rel), "dst": to_dst[step]},
            )
        )
    enc_v[...] = feats

    loads[3].wait()
    loads[5].wait()
    weights = []
    blocks = [[bw_v[r * per_row + i].astype(BF16) for i in range(per_row)] for r in range(n_src)]
    for step in range(n_dst):
        c = from_dst[step]
        for r in range(n_src):
            total = None
            for i in range(per_row):
                term = jnp.where(cols[r * per_row + i] == c, blocks[r][i], jnp.zeros_like(blocks[r][i]))
                total = term if total is None else total + term
            dense[c, core, r] = total
        weights.append(
            start(
                remote(
                    dense.at[c, core], dense.at[c, core], w_send.at[step], w_recv.at[step], {"src": partner}
                )
            )
        )
    loads[4].wait()
    if hops > 1:
        noise_copy = start(
            remote(
                noise_v.at[pl.ds(0, last), :, lanes(1 - core)],
                noise_p,
                p_send.at[3 * hops],
                p_recv.at[3 * hops],
                {"src": partner},
            )
        )

    ones = jnp.ones((8, half), BF16)

    def row_sums(z):
        squares = z * z
        high = squares.astype(BF16)
        low = (squares - high.astype(F32)).astype(BF16)
        dims = (((1,), (1,)), ((), ()))
        return lax.dot_general(ones, high, dims, preferred_element_type=F32) + lax.dot_general(
            ones, low, dims, preferred_element_type=F32
        )

    data = {}
    scales = {}
    pending = None
    kept_copies = []
    scatter_steps = list(reversed(range(1, pairs))) + [0]
    for hop in range(hops):
        for step in range(n_dst):
            c = from_dst[step]
            if hop == 0:
                weights[step].wait_recv()
            else:
                if step:
                    scales[hop, step].wait_recv()
                by = jnp.concatenate([scale[hop - 1, c, 0, 0:1], scale[hop - 1, c, 1, 0:1]], axis=1)
                for r in range(n_src):
                    w = jnp.concatenate([dense[c, 0, r], dense[c, 1, r]], axis=1)
                    scaled[r] = (w.astype(F32) * by).astype(BF16)
            for u in (0, 1):
                if hop == 0:
                    if step or u:
                        first[step, u].wait_recv()
                elif step:
                    data[hop, step, u].wait_recv()
            f = jnp.concatenate([gath[hop, c, 0], gath[hop, c, 1]], axis=0)

            def product(r):
                w = scaled[r] if hop else jnp.concatenate([dense[c, 0, r], dense[c, 1, r]], axis=1)
                return jnp.dot(w, f, preferred_element_type=F32)

            if step < n_dst - 1:
                for r in range(n_src):
                    y = product(r)
                    acc[r] = y if step == 0 else acc[r] + y
            if step == 0 and pending is not None:
                pending()
                pending = None
        copies = {}
        for u in (0, 1):
            for step in scatter_steps:
                to = to_pair[step]
                if hop < last:
                    r = to * 2 + u
                    y = product(r) + acc[r]
                    if step == 0:
                        near_in[u] = y
                        continue
                    out[hop, step - 1, u] = y.astype(BF16)
                    copies[step, u] = start(
                        remote(
                            out.at[hop, step - 1, u],
                            inn.at[hop, step - 1, u],
                            r_send.at[hop, step - 1, u],
                            r_recv.at[hop, step - 1, u],
                            {"src": at_core(to, 0)},
                        )
                    )
                    continue
                rel = u
                r = at_core(to, rel)
                y = product(r) + acc[r]
                if step == 0 and rel == 0:
                    ends[core] = y
                elif step == 0:
                    near_out[...] = y
                    copies[0, 1] = start(
                        remote(
                            near_out, ends.at[core], p_send.at[3 * hops + 1], p_recv.at[3 * hops + 1], {"src": partner}
                        )
                    )
                else:
                    out[hop, step - 1, rel] = y.astype(BF16)
                    copies[step, rel] = start(
                        remote(
                            out.at[hop, step - 1, rel],
                            inn.at[hop, step - 1, core],
                            r_send.at[hop, step - 1, rel],
                            r_recv.at[hop, step - 1, rel],
                            {"src": r},
                        )
                    )
        if hop == last:
            copies[0, 1].wait_recv()
            sums = [ends[h] + noise_v[hop, :, h * half : (h + 1) * half].astype(F32) for h in range(2)]
            for rel in (0, 1):
                for step in scatter_steps[:-1]:
                    copies[step, rel].wait_recv()
                    if rel:
                        for h in range(2):
                            sums[h] = sums[h] + inn[hop, step - 1, h].astype(F32)
            hops_v[hop] = normalized(jnp.concatenate(sums, axis=1))
            continue
        if hop == 0:
            noise_copy.wait_recv()
        z_values = []
        for u in (0, 1):
            own_noise = noise_v[hop, :, lanes(core)]
            z = near_in[u] + jnp.where(core == u, own_noise, noise_p[hop]).astype(F32)
            for step in range(1, pairs):
                copies[step, u].wait_recv()
                z = z + inn[hop, step - 1, u].astype(F32)
            gath[hop + 1, dst, u] = z.astype(BF16)
            for step in middle + rest:
                data[hop + 1, step, u] = start(
                    remote(
                        gath.at[hop + 1, dst, u],
                        gath.at[hop + 1, dst, u],
                        g_send.at[hop + 1, step, u],
                        g_recv.at[hop + 1, step, u],
                        {"dst": to_dst[step]},
                    )
                )
            zs[u] = z
            stat_out[hop, u] = row_sums(z)
        stats = start(
            remote(stat_out.at[hop], stat_in.at[hop], p_send.at[hop], p_recv.at[hop], {"src": partner})
        )
        stats.wait_recv()
        scale[hop, dst] = lax.rsqrt((stat_out[hop] + stat_in[hop]) * (1.0 / width) + 1e-06)
        for step in far_first:
            scales[hop + 1, step] = start(
                remote(
                    scale.at[hop, dst],
                    scale.at[hop, dst],
                    s_send.at[hop, step],
                    s_recv.at[hop, step],
                    {"dst": to_dst[step]},
                )
            )

        def pending(hop=hop):
            for u in (0, 1):
                column = jnp.transpose(jnp.broadcast_to(scale[hop, dst, u, 0:1], (rows, rows)))
                kept[hop, u] = (zs[u] * column).astype(BF16)
            hops_v[hop, :, lanes(core)] = kept[hop, core]
            kept_copies.append(
                start(
                    remote(
                        kept.at[hop, 1 - core],
                        kept_in.at[hop],
                        p_send.at[hops + hop],
                        p_recv.at[hops + hop],
                        {"src": partner},
                    )
                )
            )

    for hop, copy in enumerate(kept_copies):
        copy.wait_recv()
        hops_v[hop, :, lanes(1 - core)] = kept_in[hop]
    for copy in sent:
        copy.wait_send()


def finish(enc_i, hops_i, enc_o, hops_o, sem):
    writes = [
        pltpu.make_async_copy(hops_i, hops_o, sem.at[0]),
        pltpu.make_async_copy(enc_i, enc_o, sem.at[1]),
    ]
    for write in writes:
        write.start()
    for write in writes:
        write.wait()


def shards(n_src, n_dst, raw, enc_w1, enc_w2, block_weights, block_cols, noise):
    blocks, side, _ = block_weights.shape
    hops, rows, width = noise.shape
    pairs = n_src // 2
    half = width // 2
    assert rows == side and n_src % 2 == 0
    anywhere = pl.BlockSpec(memory_space=pl.ANY)
    inside = pl.BlockSpec(memory_space=pltpu.VMEM)
    dma = pltpu.SemaphoreType.DMA
    far = max(pairs - 1, 1)
    mid = max(hops - 1, 1)
    encoded, kept = pl.pallas_call(
        functools.partial(kernel, n_src, n_dst, hops),
        out_shape=(pltpu.VMEM((rows, width), BF16), pltpu.VMEM((hops, rows, width), BF16)),
        in_specs=[anywhere] * 6,
        out_specs=(inside, inside),
        scratch_shapes=[
            pltpu.VMEM(raw.shape, BF16),
            pltpu.VMEM(enc_w1.shape, BF16),
            pltpu.VMEM(enc_w2.shape, BF16),
            pltpu.VMEM(block_weights.shape, F32),
            pltpu.VMEM(noise.shape, BF16),
            pltpu.SMEM(block_cols.shape, jnp.int32),
            pltpu.VMEM((n_dst, 2, n_src, side, side), BF16),
            pltpu.VMEM((n_src, side, 2 * side), BF16),
            pltpu.VMEM((hops, n_dst, 2, rows, half), BF16),
            pltpu.VMEM((rows, half), BF16),
            pltpu.VMEM((n_src, rows, half), F32),
            pltpu.VMEM((hops, far, 2, rows, half), BF16),
            pltpu.VMEM((hops, far, 2, rows, half), BF16),
            pltpu.VMEM((rows, half), F32),
            pltpu.VMEM((2, rows, half), F32),
            pltpu.VMEM((mid, rows, half), BF16),
            pltpu.VMEM((2, rows, half), F32),
            pltpu.VMEM((2, rows, half), F32),
            pltpu.VMEM((mid, 2, 8, rows), F32),
            pltpu.VMEM((mid, 2, 8, rows), F32),
            pltpu.VMEM((mid, n_dst, 2, 8, rows), F32),
            pltpu.VMEM((mid, 2, rows, half), BF16),
            pltpu.VMEM((mid, rows, half), BF16),
            dma((6,)),
            dma((n_dst,)),
            dma((n_dst,)),
            dma((hops, n_dst, 2)),
            dma((hops, n_dst, 2)),
            dma((hops, far, 2)),
            dma((hops, far, 2)),
            dma((mid, n_dst)),
            dma((mid, n_dst)),
            dma((3 * hops + 2,)),
            dma((3 * hops + 2,)),
        ],
        compiler_params=pltpu.CompilerParams(
            collective_id=0, has_side_effects=True, vmem_limit_bytes=60 * 1024 * 1024
        ),
    )(raw, enc_w1, enc_w2, block_weights, block_cols, noise)
    shapes = (
        jax.ShapeDtypeStruct((rows, width), BF16),
        jax.ShapeDtypeStruct((hops, rows, width), BF16),
    )
    return pl.pallas_call(
        finish,
        out_shape=shapes,
        in_specs=[inside, inside],
        out_specs=(anywhere, anywhere),
        scratch_shapes=[dma((2,))],
    )(*(pltpu.with_memory_space_constraint(a, pltpu.VMEM) for a in (encoded, kept)))


def solution(mesh):
    placed = (
        P(("src", "dst"), None),
        P(),
        P(),
        P(("src", "dst"), None, None),
        P(("src", "dst")),
        P(None, ("src", "dst"), None),
    )
    return jax.shard_map(
        functools.partial(shards, mesh.shape["src"], mesh.shape["dst"]),
        mesh=mesh,
        in_specs=placed,
        out_specs=(P(("src", "dst"), None), P(None, ("src", "dst"), None)),
        check_vma=False,
    )
```

```python
import functools

import jax
import jax.numpy as jnp
from jax import lax
from jax.experimental import pallas as pl
from jax.experimental.pallas import tpu as pltpu
from jax.sharding import PartitionSpec as P

MESH = pl.DeviceIdType.MESH
F32 = jnp.float32
BF16 = jnp.bfloat16


def shifted(me, step, count):
    if count & (count - 1) == 0:
        return me ^ step, me ^ step
    return lax.rem(me + step, count), lax.rem(me + count - step, count)


def kernel(
    n_src, n_dst, hops,
    raw_h, w1_h, w2_h, bw_h, cols_h, noise_h,
    enc_v, hops_v,
    raw_v, w1_v, w2_v, bw_v, noise_v, cols,
    dense, scaled, gath, cross, acc, out, inn, near_out, near_in,
    noise_p, zs, ends, stat_out, stat_in, scale, kept, kept_in,
    load_sem, w_send, w_recv, g_send, g_recv, r_send, r_recv, s_send, s_recv, p_send, p_recv,
):
    src, dst = lax.axis_index("src"), lax.axis_index("dst")
    pairs = n_src // 2
    pair, core = src // 2, lax.rem(src, 2)
    partner = pair * 2 + 1 - core
    side = bw_v.shape[1]
    per_row = bw_v.shape[0] // n_src
    rows, width = enc_v.shape
    half = width // 2
    last = hops - 1

    def at_core(chip, rel):
        return chip * 2 + (1 - core if rel else core)

    def lanes(h):
        return pl.ds(pl.multiple_of(h * half, half), half)

    def remote(a, b, send, recv, to):
        return pltpu.make_async_remote_copy(
            src_ref=a, dst_ref=b, send_sem=send, recv_sem=recv, device_id=to, device_id_type=MESH
        )

    loads = [
        pltpu.make_async_copy(a, b, load_sem.at[i])
        for i, (a, b) in enumerate(
            (
                (raw_h, raw_v),
                (w1_h, w1_v),
                (w2_h, w2_v),
                (bw_h, bw_v),
                (noise_h, noise_v),
                (cols_h, cols),
            )
        )
    ]
    for load in loads:
        load.start()

    to_dst = [shifted(dst, step, n_dst)[0] if step else dst for step in range(n_dst)]
    from_dst = [shifted(dst, step, n_dst)[1] if step else dst for step in range(n_dst)]
    to_pair = [shifted(pair, step, pairs)[0] if step else pair for step in range(pairs)]

    barrier = pltpu.get_barrier_semaphore()
    greeted = 0
    greet = [{"src": partner}]
    for rel in (0, 1):
        greet += [{"src": at_core(pair, rel), "dst": to} for to in to_dst[1:]]
        greet += [{"src": at_core(to, rel)} for to in to_pair[1:]]
    for to in greet:
        pl.semaphore_signal(barrier, inc=1, device_id=to, device_id_type=MESH)
        greeted += 1

    def normalized(z):
        root = lax.rsqrt(jnp.sum(z * z, axis=-1, keepdims=True) * (1.0 / width) + 1e-06)
        return (z * root).astype(BF16)

    sent = []

    def start(copy):
        copy.start()
        sent.append(copy)
        return copy

    middle = [n_dst // 2] if n_dst > 1 else []
    rest = [step for step in range(1, n_dst) if step not in middle]
    far_first = list(reversed(range(1, n_dst)))

    loads[0].wait()
    loads[1].wait()
    v = jnp.dot(raw_v[...], w1_v[...], preferred_element_type=F32)
    hidden = (v * jax.nn.sigmoid(v)).astype(BF16)
    loads[2].wait()
    feats = normalized(jnp.dot(hidden, w2_v[...], preferred_element_type=F32))
    mine = jnp.where(core == 0, feats[:, :half], feats[:, half:])
    gath[0, dst, core] = mine
    cross[...] = jnp.where(core == 0, feats[:, half:], feats[:, :half])
    pl.semaphore_wait(barrier, greeted)
    first = {}
    for step, rel in [(step, rel) for step in middle + rest[::-1] for rel in (1, 0)] + [(0, 1)]:
        first[step, rel] = start(
            remote(
                cross if rel else gath.at[0, dst, core],
                gath.at[0, dst, core],
                g_send.at[0, step, rel],
                g_recv.at[0, step, rel],
                {"src": at_core(pair, rel), "dst": to_dst[step]},
            )
        )
    enc_v[...] = feats

    loads[3].wait()
    loads[5].wait()
    weights = []
    blocks = [[bw_v[r * per_row + i].astype(BF16) for i in range(per_row)] for r in range(n_src)]
    for step in range(n_dst):
        c = from_dst[step]
        for r in range(n_src):
            total = None
            for i in range(per_row):
                term = jnp.where(cols[r * per_row + i] == c, blocks[r][i], jnp.zeros_like(blocks[r][i]))
                total = term if total is None else total + term
            dense[c, core, r] = total
        weights.append(
            start(
                remote(
                    dense.at[c, core], dense.at[c, core], w_send.at[step], w_recv.at[step], {"src": partner}
                )
            )
        )
    loads[4].wait()
    if hops > 1:
        noise_copy = start(
            remote(
                noise_v.at[pl.ds(0, last), :, lanes(1 - core)],
                noise_p,
                p_send.at[3 * hops],
                p_recv.at[3 * hops],
                {"src": partner},
            )
        )

    ones = jnp.ones((8, half), BF16)

    def row_sums(z):
        squares = z * z
        high = squares.astype(BF16)
        low = (squares - high.astype(F32)).astype(BF16)
        dims = (((1,), (1,)), ((), ()))
        return lax.dot_general(ones, high, dims, preferred_element_type=F32) + lax.dot_general(
            ones, low, dims, preferred_element_type=F32
        )

    data = {}
    scales = {}
    pending = None
    kept_copies = []
    scatter_steps = list(reversed(range(1, pairs))) + [0]
    for hop in range(hops):
        for step in range(n_dst):
            c = from_dst[step]
            if hop == 0:
                weights[step].wait_recv()
            else:
                if step:
                    scales[hop, step].wait_recv()
                by = jnp.concatenate([scale[hop - 1, c, u : u + 1] for u in (0, 1)], axis=1)
                for r in range(n_src):
                    w = jnp.concatenate([dense[c, 0, r], dense[c, 1, r]], axis=1)
                    scaled[r] = (w.astype(F32) * by).astype(BF16)
            for u in (0, 1):
                if hop == 0:
                    if step or u:
                        first[step, u].wait_recv()
                elif step:
                    data[hop, step, u].wait_recv()
            f = jnp.concatenate([gath[hop, c, 0], gath[hop, c, 1]], axis=0)

            def product(r):
                w = scaled[r] if hop else jnp.concatenate([dense[c, 0, r], dense[c, 1, r]], axis=1)
                return jnp.dot(w, f, preferred_element_type=F32)

            if step < n_dst - 1:
                for r in range(n_src):
                    y = product(r)
                    acc[r] = y if step == 0 else acc[r] + y
            if step == 0 and pending is not None:
                pending()
                pending = None
        copies = {}
        for u in (0, 1):
            for step in scatter_steps:
                to = to_pair[step]
                if hop < last:
                    r = to * 2 + u
                    y = product(r) + acc[r]
                    if step == 0:
                        near_in[u] = y
                        continue
                    out[hop, step - 1, u] = y.astype(BF16)
                    copies[step, u] = start(
                        remote(
                            out.at[hop, step - 1, u],
                            inn.at[hop, step - 1, u],
                            r_send.at[hop, step - 1, u],
                            r_recv.at[hop, step - 1, u],
                            {"src": at_core(to, 0)},
                        )
                    )
                    continue
                rel = u
                r = at_core(to, rel)
                y = product(r) + acc[r]
                if step == 0 and rel == 0:
                    ends[core] = y
                elif step == 0:
                    near_out[...] = y
                    copies[0, 1] = start(
                        remote(
                            near_out, ends.at[core], p_send.at[3 * hops + 1], p_recv.at[3 * hops + 1], {"src": partner}
                        )
                    )
                else:
                    out[hop, step - 1, rel] = y.astype(BF16)
                    copies[step, rel] = start(
                        remote(
                            out.at[hop, step - 1, rel],
                            inn.at[hop, step - 1, core],
                            r_send.at[hop, step - 1, rel],
                            r_recv.at[hop, step - 1, rel],
                            {"src": r},
                        )
                    )
        if hop == last:
            copies[0, 1].wait_recv()
            sums = [ends[h] + noise_v[hop, :, h * half : (h + 1) * half].astype(F32) for h in range(2)]
            for rel in (0, 1):
                for step in scatter_steps[:-1]:
                    copies[step, rel].wait_recv()
                    if rel:
                        for h in range(2):
                            sums[h] = sums[h] + inn[hop, step - 1, h].astype(F32)
            hops_v[hop] = normalized(jnp.concatenate(sums, axis=1))
            continue
        if hop == 0:
            noise_copy.wait_recv()
        z_values = []
        totals = []
        for u in (0, 1):
            own_noise = noise_v[hop, :, lanes(core)]
            z = near_in[u] + jnp.where(core == u, own_noise, noise_p[hop]).astype(F32)
            for step in range(1, pairs):
                copies[step, u].wait_recv()
                z = z + inn[hop, step - 1, u].astype(F32)
            gath[hop + 1, dst, u] = z.astype(BF16)
            for step in middle + rest:
                data[hop + 1, step, u] = start(
                    remote(
                        gath.at[hop + 1, dst, u],
                        gath.at[hop + 1, dst, u],
                        g_send.at[hop + 1, step, u],
                        g_recv.at[hop + 1, step, u],
                        {"dst": to_dst[step]},
                    )
                )
            zs[u] = z
            totals.append(row_sums(z))
        first_row = lax.broadcasted_iota(jnp.int32, totals[0].shape, 0) == 0
        stat_out[hop] = jnp.where(first_row, totals[0], totals[1])
        stats = start(
            remote(stat_out.at[hop], stat_in.at[hop], p_send.at[hop], p_recv.at[hop], {"src": partner})
        )
        stats.wait_recv()
        scale[hop, dst] = lax.rsqrt((stat_out[hop] + stat_in[hop]) * (1.0 / width) + 1e-06)
        for step in far_first:
            scales[hop + 1, step] = start(
                remote(
                    scale.at[hop, dst],
                    scale.at[hop, dst],
                    s_send.at[hop, step],
                    s_recv.at[hop, step],
                    {"dst": to_dst[step]},
                )
            )

        def pending(hop=hop):
            for u in (0, 1):
                column = jnp.transpose(jnp.broadcast_to(scale[hop, dst, u : u + 1], (rows, rows)))
                kept[hop, u] = (zs[u] * column).astype(BF16)
            hops_v[hop, :, lanes(core)] = kept[hop, core]
            kept_copies.append(
                start(
                    remote(
                        kept.at[hop, 1 - core],
                        kept_in.at[hop],
                        p_send.at[hops + hop],
                        p_recv.at[hops + hop],
                        {"src": partner},
                    )
                )
            )

    for hop, copy in enumerate(kept_copies):
        copy.wait_recv()
        hops_v[hop, :, lanes(1 - core)] = kept_in[hop]
    for copy in sent:
        copy.wait_send()


def finish(enc_i, hops_i, enc_o, hops_o, sem):
    writes = [
        pltpu.make_async_copy(hops_i, hops_o, sem.at[0]),
        pltpu.make_async_copy(enc_i, enc_o, sem.at[1]),
    ]
    for write in writes:
        write.start()
    for write in writes:
        write.wait()


def shards(n_src, n_dst, raw, enc_w1, enc_w2, block_weights, block_cols, noise):
    blocks, side, _ = block_weights.shape
    hops, rows, width = noise.shape
    pairs = n_src // 2
    half = width // 2
    assert rows == side and n_src % 2 == 0
    anywhere = pl.BlockSpec(memory_space=pl.ANY)
    inside = pl.BlockSpec(memory_space=pltpu.VMEM)
    dma = pltpu.SemaphoreType.DMA
    far = max(pairs - 1, 1)
    mid = max(hops - 1, 1)
    encoded, kept = pl.pallas_call(
        functools.partial(kernel, n_src, n_dst, hops),
        out_shape=(pltpu.VMEM((rows, width), BF16), pltpu.VMEM((hops, rows, width), BF16)),
        in_specs=[anywhere] * 6,
        out_specs=(inside, inside),
        scratch_shapes=[
            pltpu.VMEM(raw.shape, BF16),
            pltpu.VMEM(enc_w1.shape, BF16),
            pltpu.VMEM(enc_w2.shape, BF16),
            pltpu.VMEM(block_weights.shape, F32),
            pltpu.VMEM(noise.shape, BF16),
            pltpu.SMEM(block_cols.shape, jnp.int32),
            pltpu.VMEM((n_dst, 2, n_src, side, side), BF16),
            pltpu.VMEM((n_src, side, 2 * side), BF16),
            pltpu.VMEM((hops, n_dst, 2, rows, half), BF16),
            pltpu.VMEM((rows, half), BF16),
            pltpu.VMEM((n_src, rows, half), F32),
            pltpu.VMEM((hops, far, 2, rows, half), BF16),
            pltpu.VMEM((hops, far, 2, rows, half), BF16),
            pltpu.VMEM((rows, half), F32),
            pltpu.VMEM((2, rows, half), F32),
            pltpu.VMEM((mid, rows, half), BF16),
            pltpu.VMEM((2, rows, half), F32),
            pltpu.VMEM((2, rows, half), F32),
            pltpu.VMEM((mid, 8, rows), F32),
            pltpu.VMEM((mid, 8, rows), F32),
            pltpu.VMEM((mid, n_dst, 8, rows), F32),
            pltpu.VMEM((mid, 2, rows, half), BF16),
            pltpu.VMEM((mid, rows, half), BF16),
            dma((6,)),
            dma((n_dst,)),
            dma((n_dst,)),
            dma((hops, n_dst, 2)),
            dma((hops, n_dst, 2)),
            dma((hops, far, 2)),
            dma((hops, far, 2)),
            dma((mid, n_dst)),
            dma((mid, n_dst)),
            dma((3 * hops + 2,)),
            dma((3 * hops + 2,)),
        ],
        compiler_params=pltpu.CompilerParams(
            collective_id=0, has_side_effects=True, vmem_limit_bytes=60 * 1024 * 1024
        ),
    )(raw, enc_w1, enc_w2, block_weights, block_cols, noise)
    shapes = (
        jax.ShapeDtypeStruct((rows, width), BF16),
        jax.ShapeDtypeStruct((hops, rows, width), BF16),
    )
    return pl.pallas_call(
        finish,
        out_shape=shapes,
        in_specs=[inside, inside],
        out_specs=(anywhere, anywhere),
        scratch_shapes=[dma((2,))],
    )(*(pltpu.with_memory_space_constraint(a, pltpu.VMEM) for a in (encoded, kept)))


def solution(mesh):
    placed = (
        P(("src", "dst"), None),
        P(),
        P(),
        P(("src", "dst"), None, None),
        P(("src", "dst")),
        P(None, ("src", "dst"), None),
    )
    return jax.shard_map(
        functools.partial(shards, mesh.shape["src"], mesh.shape["dst"]),
        mesh=mesh,
        in_specs=placed,
        out_specs=(P(("src", "dst"), None), P(None, ("src", "dst"), None)),
        check_vma=False,
    )
```
